32 devices in a mesh: col: 4 (over y, x), row: 8 (over z, core).
Axes of the slice: x: 2, y: 2, z: 4, core: 2. Of those that a mesh axis runs over, the one named last changes fastest.
Arguments:
- upper_blocks: float32 [4096, 512], P('row', 'col'), may hold values from -40 to 40
- lower_blocks: float32 [4096, 512], P('row', 'col'), may hold values from -40 to 40
Outputs:
- upper_rotated: float32 [4096, 512], P('row', 'col')
- lower_rotated: float32 [4096, 512], P('row', 'col')
The draws below stay inside these ranges and needn't reach their ends.
All inputs are finite; a program needn't handle non-finite values.
Results may differ from the reference program's by a relative error of at most 0.0001.
Values sent between devices are 32-bit elements; how exact they have to be, the bound alone decides.
A program may use at most 64 MiB of HBM per device.

```python
import math
import jax
import jax.numpy as jnp
from jax import lax

BLOCK = 128
ROUNDS = 2
HALF = 512
COLS = 1024
ROWS = 4096
N_COL = 4


def whole_matrix(key):
    base = jax.random.fold_in(key, 11)
    keys = jax.random.split(base, 4)
    noise = jax.random.normal(keys[0], (ROWS, COLS), jnp.float32)
    mixing = jnp.eye(COLS, dtype=jnp.float32) + 0.7 * jax.random.normal(keys[1], (COLS, COLS), jnp.float32) / math.sqrt(COLS)
    mixed = jnp.dot(noise, mixing, precision=lax.Precision.HIGHEST)
    column_scale = jnp.exp(jax.random.uniform(keys[2], (COLS,), jnp.float32, math.log(0.3), math.log(3.0)))
    position = jnp.arange(ROWS, dtype=jnp.float32) / ROWS
    row_scale = jnp.exp(math.log(3.0) * position + jax.random.uniform(keys[3], (ROWS,), jnp.float32, -0.35, 0.35))
    return jnp.clip(mixed * row_scale[:, None] * column_scale[None, :] / 1.7, -40.0, 40.0)


def draw_upper_blocks(key, part):
    return whole_matrix(key)[:, :HALF]


def draw_lower_blocks(key, part):
    return whole_matrix(key)[:, HALF:]


def setup_inputs(seed: int = 0) -> dict:
    splits = jax.random.split(jax.random.key(seed), 3)
    return {
        "upper_blocks": draw_upper_blocks(jax.random.fold_in(splits[2], 71), 0),
        "lower_blocks": draw_lower_blocks(jax.random.fold_in(splits[2], 71), 0),
    }


def couple(cross_gram, upper_norms, lower_norms):
    column_gap = upper_norms[..., :, None] - lower_norms[..., None, :]
    column_sum = upper_norms[..., :, None] + lower_norms[..., None, :]
    return -cross_gram * column_gap / (2.0 * column_gap * column_gap + 0.5 * column_sum * column_sum + 1e-05)

def rotation(coupling):
    identity = jnp.eye(coupling.shape[0], dtype=coupling.dtype)
    outer_gram = jnp.dot(coupling, coupling.T, precision=lax.Precision.HIGHEST)
    inner_gram = jnp.dot(coupling.T, coupling, precision=lax.Precision.HIGHEST)
    left_factor = jnp.linalg.cholesky(identity + outer_gram)
    right_factor = jnp.linalg.cholesky(identity + inner_gram)
    keep_upper = jax.scipy.linalg.cho_solve((left_factor, True), identity - outer_gram)
    upper_to_lower = jax.scipy.linalg.cho_solve((left_factor, True), 2.0 * coupling)
    lower_to_upper = jax.scipy.linalg.cho_solve((right_factor, True), -2.0 * coupling.T)
    keep_lower = jax.scipy.linalg.cho_solve((right_factor, True), identity - inner_gram)
    return (keep_upper, upper_to_lower, lower_to_upper, keep_lower)

def reference(upper_blocks, lower_blocks):
    upper = upper_blocks.reshape(ROWS, N_COL, BLOCK)
    lower = lower_blocks.reshape(ROWS, N_COL, BLOCK)
    highest = lax.Precision.HIGHEST
    for round_index in range(ROUNDS):
        cross_gram = jnp.einsum('mcb,mcd->cbd', upper, lower, precision=highest) / ROWS
        upper_norms = jnp.sum(upper * upper, axis=0) / ROWS
        lower_norms = jnp.sum(lower * lower, axis=0) / ROWS
        coupling = couple(cross_gram, upper_norms, lower_norms)
        keep_upper, upper_to_lower, lower_to_upper, keep_lower = jax.vmap(rotation)(coupling)
        new_upper = jnp.einsum('mcb,cbd->mcd', upper, keep_upper, precision=highest) + jnp.einsum('mcb,cbd->mcd', lower, lower_to_upper, precision=highest)
        new_lower = jnp.einsum('mcb,cbd->mcd', upper, upper_to_lower, precision=highest) + jnp.einsum('mcb,cbd->mcd', lower, keep_lower, precision=highest)
        if round_index + 1 < ROUNDS:
            upper = jnp.roll(new_upper, 1, axis=1)
            lower = jnp.roll(new_lower, -1, axis=1)
        else:
            upper = new_upper
            lower = new_lower
    return (upper.reshape(ROWS, HALF), lower.reshape(ROWS, HALF))
```

```python
import functools

import jax
import jax.numpy as jnp
from jax import lax
from jax.experimental import pallas as pl
from jax.experimental.pallas import tpu as pltpu
from jax.sharding import PartitionSpec as P

ROUNDS = 2
CHUNKS = 4
MESH = pl.DeviceIdType.MESH
F32 = jnp.float32
BF16 = jnp.bfloat16
HIGHEST = lax.Precision.HIGHEST


def split(x):
    high = x.astype(BF16)
    low = (x - high.astype(F32)).astype(BF16)
    return high, low


def exact_dot(a, b, contract=(1, 0)):
    dims = (((contract[0],), (contract[1],)), ((), ()))
    return lax.dot_general(a, b, dims, precision=HIGHEST, preferred_element_type=F32)


def fast_dot(a, b):
    return jnp.dot(a, b, preferred_element_type=F32)


def gram(upper, lower):
    width = upper.shape[1]
    left = jnp.concatenate(split(upper), axis=1)
    right = jnp.concatenate(split(lower), axis=1)
    q = lax.dot_general(
        left, right, (((0,), (0,)), ((), ())), preferred_element_type=F32
    )
    return q[:width, :width] + (q[:width, width:] + q[width:, :width])


def step_count(width):
    square = (width / 4.0) ** 2
    spread = 0.5 * square / (1.0 + 0.5 * square)
    steps = 0
    while spread > 1e-3:
        spread = spread * spread / (2.0 - spread * spread)
        steps += 1
    return steps


def rotation(p):
    width = p.shape[0]
    rows = lax.broadcasted_iota(jnp.int32, (width, width), 0)
    lanes = lax.broadcasted_iota(jnp.int32, (width, width), 1)
    eye = (rows == lanes).astype(F32)
    s = exact_dot(p, p, (1, 1))
    total = jnp.sum(jnp.sum(p * p, axis=0, keepdims=True), axis=1, keepdims=True)
    total = jnp.broadcast_to(total, (1, width))
    scale = 1.0 / (1.0 + 0.5 * total)
    spread = 0.5 * total * scale
    e = spread * eye - scale * s
    x = None
    steps = step_count(width)
    for step in range(steps):
        square = spread * spread
        gain = 2.0 / (2.0 - square)
        spread = 0.5 * square * gain
        if step == 0:
            x = (gain * scale) * (eye + e)
            squared = exact_dot(e, e)
        elif step < steps - 1:
            y = exact_dot(jnp.concatenate([x, e], axis=0), e)
            x = gain * (x + y[:width])
            squared = y[width:]
        else:
            x = gain * (x + exact_dot(x, e))
        if step < steps - 1:
            e = gain * squared - spread * eye
    e = (eye - x) - exact_dot(s, x)
    x = x + exact_dot(x, e)
    ap = exact_dot(x, p)
    cross = 2.0 * ap
    keep_upper = 2.0 * x - eye
    keep_lower = eye - exact_dot(p, cross, (0, 0))
    top = jnp.concatenate([keep_upper, cross], axis=1)
    bottom = jnp.concatenate([-cross.T, keep_lower], axis=1)
    return jnp.concatenate([top, bottom], axis=0)


def turn(upper, lower, parts):
    high, low = split(jnp.concatenate([upper, lower], axis=1))
    w_high, w_low = parts
    return fast_dot(high, w_high) + (fast_dot(low, w_high) + fast_dot(high, w_low))


def kernel(
    n_row, n_col, upper_ref, lower_ref, out_upper, out_lower,
    swapped, work, gram_out, gram_in, line_out, line_in, pair,
    swap_send, swap_recv, gram_send, gram_recv, line_send, line_recv,
    pair_send, pair_recv, shift_send, shift_recv,
):
    depth, width = upper_ref.shape
    half = width // 2
    chunk = depth // CHUNKS
    n_line = n_row // 2
    row_total = float(depth * n_row)
    row, col = lax.axis_index("row"), lax.axis_index("col")
    core = lax.rem(row, 2)
    chip_row = row - core
    partner = chip_row + 1 - core
    odd = lax.rem(col, 2)
    beside = col + 1 - 2 * odd
    ahead = lax.rem(col + 2, n_col)
    behind = lax.rem(col + n_col - 2, n_col)
    shift_to = ahead + odd * (behind - ahead)

    def line_row(k):
        return lax.rem(row + 2 * k, n_row)

    barrier = pltpu.get_barrier_semaphore()
    greeted = [(chip_row, beside), (chip_row + 1, beside), (partner, col)]
    greeted += [(line_row(k), col) for k in range(1, n_line)]
    greeted += [(row, ahead)] + ([] if n_col == 4 else [(row, behind)])
    for r, c in greeted:
        pl.semaphore_signal(barrier, inc=1, device_id={"row": r, "col": c}, device_id_type=MESH)

    def remote(src, dst, send, recv, r, c):
        return pltpu.make_async_remote_copy(
            src_ref=src, dst_ref=dst, send_sem=send, recv_sem=recv,
            device_id={"row": r, "col": c}, device_id_type=MESH,
        )

    def put_statistics(index, g, upper_sums, lower_sums):
        which = lax.broadcasted_iota(jnp.int32, (8, width), 0)
        norms = jnp.where(which == 0, upper_sums, jnp.where(which == 1, lower_sums, 0.0))
        for k in range(2):
            gram_out[index, k, :half, :] = g[k * half : (k + 1) * half]
            gram_out[index, k, half:, :] = norms

    def reduce_line(index, own):
        line_out[index] = own
        copies = []
        for k in range(1, n_line):
            copies.append(
                remote(
                    line_out.at[index], line_in.at[index, k - 1],
                    line_send.at[index, k - 1], line_recv.at[index, k - 1], line_row(k), col,
                )
            )
            copies[-1].start()
        total = own
        for k in range(1, n_line):
            copies[k - 1].wait_recv()
            total = total + line_in[index, k - 1]
        return total, copies

    def coupling(index, total):
        total = total / row_total
        a_row, b = total[half : half + 1], total[half + 1 : half + 2]
        i = lax.broadcasted_iota(jnp.int32, (half, width), 0) + core * half
        j = lax.broadcasted_iota(jnp.int32, (half, width), 1)
        a = jnp.sum(jnp.where(i == j, a_row, 0.0), axis=1, keepdims=True)
        gap, both = a - b, a + b
        share = -total[:half] * gap / (2.0 * gap * gap + 0.5 * both * both + 1e-05)
        pair[index, core] = share
        copy = remote(
            pair.at[index, core], pair.at[index, core],
            pair_send.at[index], pair_recv.at[index], partner, col,
        )
        copy.start()
        copy.wait_recv()
        return pair[index].reshape(width, width), copy

    pending = []

    upper, lower = upper_ref[...], lower_ref[...]
    put_statistics(
        0, gram(upper, lower),
        jnp.sum(upper * upper, axis=0, keepdims=True), jnp.sum(lower * lower, axis=0, keepdims=True),
    )
    pl.semaphore_wait(barrier, len(greeted))

    copies = []
    for k in range(2):
        copies.append(
            remote(
                gram_out.at[0, k], gram_in.at[core], gram_send.at[k], gram_recv.at[core],
                chip_row + k, beside,
            )
        )
        copies[-1].start()
    pending += copies
    swaps = []
    for i in range(CHUNKS):
        rows = pl.ds(i * chunk, chunk)
        for which, ref in enumerate((upper_ref, lower_ref)):
            swaps.append(
                remote(
                    ref.at[rows], swapped.at[which, rows],
                    swap_send.at[which, i], swap_recv.at[which, i], row, beside,
                )
            )
            swaps[-1].start()
    pending += swaps
    for k in range(2):
        pltpu.make_async_remote_copy(
            src_ref=gram_out.at[0, k], dst_ref=gram_in.at[k], send_sem=gram_send.at[k],
            recv_sem=gram_recv.at[k], device_id={"row": row, "col": beside}, device_id_type=MESH,
        ).wait_recv()
    total, copies = reduce_line(0, gram_in[0] + gram_in[1])
    pending += copies
    p, copy = coupling(0, total)
    pending.append(copy)
    parts = split(rotation(p))

    shifts = []
    for i in range(CHUNKS):
        rows = pl.ds(i * chunk, chunk)
        swaps[2 * i].wait_recv()
        swaps[2 * i + 1].wait_recv()
        y = turn(swapped[0, rows, :], swapped[1, rows, :], parts)
        work[0, rows, :] = y[:, :width]
        work[1, rows, :] = y[:, width:]
        shifts.append(
            remote(
                work.at[odd, rows], work.at[2, rows], shift_send.at[i], shift_recv.at[i],
                row, shift_to,
            )
        )
        shifts[-1].start()
    pending += shifts

    upper_slot, lower_slot = 2 - 2 * odd, 1 + odd
    g, upper_sums, lower_sums = 0.0, 0.0, 0.0
    for i in range(CHUNKS):
        rows = pl.ds(i * chunk, chunk)
        shifts[i].wait_recv()
        upper, lower = work[upper_slot, rows, :], work[lower_slot, rows, :]
        g = g + gram(upper, lower)
        upper_sums = upper_sums + jnp.sum(upper * upper, axis=0, keepdims=True)
        lower_sums = lower_sums + jnp.sum(lower * lower, axis=0, keepdims=True)
    put_statistics(1, g, upper_sums, lower_sums)
    copy = remote(
        gram_out.at[1, 1 - core], gram_in.at[2], gram_send.at[2], gram_recv.at[2], partner, col
    )
    copy.start()
    pending.append(copy)
    copy.wait_recv()
    total, copies = reduce_line(1, gram_out[1, core] + gram_in[2])
    pending += copies
    p, copy = coupling(1, total)
    pending.append(copy)
    parts = split(rotation(p))
    for i in range(CHUNKS):
        rows = pl.ds(i * chunk, chunk)
        y = turn(work[upper_slot, rows, :], work[lower_slot, rows, :], parts)
        out_upper[rows, :] = y[:, :width]
        out_lower[rows, :] = y[:, width:]
    for copy in pending:
        copy.wait_send()


def shards(n_row, n_col, upper_blocks, lower_blocks):
    depth, width = upper_blocks.shape
    half = width // 2
    n_line = n_row // 2
    out = jax.ShapeDtypeStruct((depth, width), F32)
    dma = pltpu.SemaphoreType.DMA
    return pl.pallas_call(
        functools.partial(kernel, n_row, n_col),
        out_shape=(out, out),
        in_specs=[pl.BlockSpec(memory_space=pltpu.VMEM)] * 2,
        out_specs=(pl.BlockSpec(memory_space=pltpu.VMEM),) * 2,
        scratch_shapes=[
            pltpu.VMEM((2, depth, width), F32),
            pltpu.VMEM((3, depth, width), F32),
            pltpu.VMEM((ROUNDS, 2, half + 8, width), F32),
            pltpu.VMEM((3, half + 8, width), F32),
            pltpu.VMEM((ROUNDS, half + 8, width), F32),
            pltpu.VMEM((ROUNDS, n_line - 1, half + 8, width), F32),
            pltpu.VMEM((ROUNDS, 2, half, width), F32),
            dma((2, CHUNKS)),
            dma((2, CHUNKS)),
            dma((3,)),
            dma((3,)),
            dma((ROUNDS, n_line - 1)),
            dma((ROUNDS, n_line - 1)),
            dma((ROUNDS,)),
            dma((ROUNDS,)),
            dma((CHUNKS,)),
            dma((CHUNKS,)),
        ],
        compiler_params=pltpu.CompilerParams(collective_id=0, has_side_effects=True),
    )(upper_blocks, lower_blocks)


def solution(mesh):
    placed = (P("row", "col"), P("row", "col"))
    return jax.shard_map(
        functools.partial(shards, mesh.shape["row"], mesh.shape["col"]),
        mesh=mesh,
        in_specs=placed,
        out_specs=(P("row", "col"), P("row", "col")),
        check_vma=False,
    )
```

```python
import functools

import jax
import jax.numpy as jnp
from jax import lax
from jax.experimental import pallas as pl
from jax.experimental.pallas import tpu as pltpu
from jax.sharding import PartitionSpec as P

ROUNDS = 2
CHUNKS = 4
MESH = pl.DeviceIdType.MESH
F32 = jnp.float32
BF16 = jnp.bfloat16


def split(x):
    high = x.astype(BF16)
    low = (x - high.astype(F32)).astype(BF16)
    return high, low


def split_three(x):
    high = x.astype(BF16)
    rest = x - high.astype(F32)
    middle = rest.astype(BF16)
    return high, middle, (rest - middle.astype(F32)).astype(BF16)


def fast_dot(a, b):
    return jnp.dot(a, b, preferred_element_type=F32)


def exact_dot(a, b):
    width = b.shape[1]
    (a0, a1, a2), (b0, b1, b2) = split_three(a), split_three(b)
    upper = jnp.concatenate([b0, b1], axis=1)
    lower = jnp.concatenate([b1, b0], axis=1)
    large = fast_dot(jnp.concatenate([a0, a1], axis=1), jnp.concatenate([upper, lower], axis=0))
    small = fast_dot(jnp.concatenate([a0, a2], axis=1), jnp.concatenate([b2, b0], axis=0))
    return large[:, :width] + (large[:, width:] + small)


def gram(upper, lower):
    width = upper.shape[1]
    left = jnp.concatenate(split(upper), axis=1)
    right = jnp.concatenate(split(lower), axis=1)
    q = lax.dot_general(
        left, right, (((0,), (0,)), ((), ())), preferred_element_type=F32
    )
    return q[:width, :width] + (q[:width, width:] + q[width:, :width])


def step_count(width):
    square = (width / 4.0) ** 2
    spread = 0.5 * square / (1.0 + 0.5 * square)
    steps = 0
    while spread > 1e-3:
        spread = spread * spread / (2.0 - spread * spread)
        steps += 1
    return steps


def rotation(p):
    width = p.shape[0]
    rows = lax.broadcasted_iota(jnp.int32, (width, width), 0)
    lanes = lax.broadcasted_iota(jnp.int32, (width, width), 1)
    eye = (rows == lanes).astype(F32)
    s = exact_dot(p, p.T)
    total = jnp.sum(jnp.sum(p * p, axis=0, keepdims=True), axis=1, keepdims=True)
    total = jnp.broadcast_to(total, (1, width))
    scale = 1.0 / (1.0 + 0.5 * total)
    spread = 0.5 * total * scale
    e = spread * eye - scale * s
    x = None
    steps = step_count(width)
    for step in range(steps):
        square = spread * spread
        gain = 2.0 / (2.0 - square)
        spread = 0.5 * square * gain
        if step == 0:
            x = (gain * scale) * (eye + e)
            squared = exact_dot(e, e)
        elif step < steps - 1:
            y = exact_dot(jnp.concatenate([x, e], axis=0), e)
            x = gain * (x + y[:width])
            squared = y[width:]
        else:
            x = gain * (x + exact_dot(x, e))
        if step < steps - 1:
            e = gain * squared - spread * eye
    e = (eye - x) - exact_dot(s, x)
    x = x + exact_dot(x, e)
    ap = exact_dot(x, p)
    cross = 2.0 * ap
    keep_upper = 2.0 * x - eye
    keep_lower = eye - exact_dot(p.T, cross)
    top = jnp.concatenate([keep_upper, cross], axis=1)
    bottom = jnp.concatenate([-cross.T, keep_lower], axis=1)
    return jnp.concatenate([top, bottom], axis=0)


def turn(upper, lower, parts):
    high, low = split(jnp.concatenate([upper, lower], axis=1))
    w_high, w_low = parts
    return fast_dot(high, w_high) + (fast_dot(low, w_high) + fast_dot(high, w_low))


def kernel(
    n_row, n_col, upper_hbm, lower_hbm, work, out_p,
    loaded, swapped, gram_out, gram_in, line_out, line_in, pair,
    swap_send, swap_recv, gram_send, gram_recv, line_send, line_recv,
    pair_send, pair_recv, shift_send, shift_recv, load_sem,
):
    depth, width = upper_hbm.shape
    upper_ref, lower_ref = loaded.at[0], loaded.at[1]
    half = width // 2
    chunk = depth // CHUNKS
    n_line = n_row // 2
    row_total = float(depth * n_row)
    row, col = lax.axis_index("row"), lax.axis_index("col")
    core = lax.rem(row, 2)
    chip_row = row - core
    partner = chip_row + 1 - core
    odd = lax.rem(col, 2)
    beside = col + 1 - 2 * odd
    ahead = lax.rem(col + 2, n_col)
    behind = lax.rem(col + n_col - 2, n_col)
    shift_to = ahead + odd * (behind - ahead)

    def line_row(k):
        return lax.rem(row + 2 * k, n_row)

    loads = []
    for i in range(CHUNKS):
        rows = pl.ds(i * chunk, chunk)
        for which, ref in enumerate((upper_hbm, lower_hbm)):
            loads.append(pltpu.make_async_copy(ref.at[rows], loaded.at[which, rows], load_sem.at[which, i]))
            loads[-1].start()
    barrier = pltpu.get_barrier_semaphore()
    greeted = [(chip_row, beside), (chip_row + 1, beside), (partner, col)]
    greeted += [(line_row(k), col) for k in range(1, n_line)]
    greeted += [(row, ahead)] + ([] if n_col == 4 else [(row, behind)])
    for r, c in greeted:
        pl.semaphore_signal(barrier, inc=1, device_id={"row": r, "col": c}, device_id_type=MESH)

    def remote(src, dst, send, recv, r, c):
        return pltpu.make_async_remote_copy(
            src_ref=src, dst_ref=dst, send_sem=send, recv_sem=recv,
            device_id={"row": r, "col": c}, device_id_type=MESH,
        )

    def put_statistics(index, g, upper_sums, lower_sums):
        which = lax.broadcasted_iota(jnp.int32, (8, width), 0)
        norms = jnp.where(which == 0, upper_sums, jnp.where(which == 1, lower_sums, 0.0))
        for k in range(2):
            gram_out[index, k, :half, :] = g[k * half : (k + 1) * half]
            gram_out[index, k, half:, :] = norms

    def reduce_line(index, own):
        line_out[index] = own
        copies = []
        for k in range(1, n_line):
            copies.append(
                remote(
                    line_out.at[index], line_in.at[index, k - 1],
                    line_send.at[index, k - 1], line_recv.at[index, k - 1], line_row(k), col,
                )
            )
            copies[-1].start()
        total = own
        for k in range(1, n_line):
            copies[k - 1].wait_recv()
            total = total + line_in[index, k - 1]
        return total, copies

    def coupling(index, total):
        total = total / row_total
        a_row, b = total[half : half + 1], total[half + 1 : half + 2]
        i = lax.broadcasted_iota(jnp.int32, (half, width), 0) + core * half
        j = lax.broadcasted_iota(jnp.int32, (half, width), 1)
        a = jnp.sum(jnp.where(i == j, a_row, 0.0), axis=1, keepdims=True)
        gap, both = a - b, a + b
        share = -total[:half] * gap / (2.0 * gap * gap + 0.5 * both * both + 1e-05)
        pair[index, core] = share
        copy = remote(
            pair.at[index, core], pair.at[index, core],
            pair_send.at[index], pair_recv.at[index], partner, col,
        )
        copy.start()
        copy.wait_recv()
        return pair[index].reshape(width, width), copy

    pending = []

    def statistics(index, fetch):
        g, upper_sums, lower_sums = 0.0, 0.0, 0.0
        for i in range(CHUNKS):
            upper, lower = fetch(i, pl.ds(i * chunk, chunk))
            g = g + gram(upper, lower)
            upper_sums = upper_sums + jnp.sum(upper * upper, axis=0, keepdims=True)
            lower_sums = lower_sums + jnp.sum(lower * lower, axis=0, keepdims=True)
        put_statistics(index, g, upper_sums, lower_sums)

    def fetch_loaded(i, rows):
        loads[2 * i].wait()
        loads[2 * i + 1].wait()
        return loaded[0, rows, :], loaded[1, rows, :]

    statistics(0, fetch_loaded)
    pl.semaphore_wait(barrier, len(greeted))

    copies = []
    for k in range(2):
        copies.append(
            remote(
                gram_out.at[0, k], gram_in.at[core], gram_send.at[k], gram_recv.at[core],
                chip_row + k, beside,
            )
        )
        copies[-1].start()
    pending += copies
    swaps = []
    for i in range(CHUNKS):
        rows = pl.ds(i * chunk, chunk)
        for which, ref in enumerate((upper_ref, lower_ref)):
            swaps.append(
                remote(
                    ref.at[rows], swapped.at[which, rows],
                    swap_send.at[which, i], swap_recv.at[which, i], row, beside,
                )
            )
            swaps[-1].start()
    pending += swaps
    for k in range(2):
        pltpu.make_async_remote_copy(
            src_ref=gram_out.at[0, k], dst_ref=gram_in.at[k], send_sem=gram_send.at[k],
            recv_sem=gram_recv.at[k], device_id={"row": row, "col": beside}, device_id_type=MESH,
        ).wait_recv()
    total, copies = reduce_line(0, gram_in[0] + gram_in[1])
    pending += copies
    p, copy = coupling(0, total)
    pending.append(copy)
    parts = split(rotation(p))

    shifts = []
    for i in range(CHUNKS):
        rows = pl.ds(i * chunk, chunk)
        swaps[2 * i].wait_recv()
        swaps[2 * i + 1].wait_recv()
        y = turn(swapped[0, rows, :], swapped[1, rows, :], parts)
        work[0, rows, :] = y[:, :width]
        work[1, rows, :] = y[:, width:]
        shifts.append(
            remote(
                work.at[odd, rows], work.at[2, rows], shift_send.at[i], shift_recv.at[i],
                row, shift_to,
            )
        )
        shifts[-1].start()
    pending += shifts

    upper_slot, lower_slot = 2 - 2 * odd, 1 + odd

    def fetch_shifted(i, rows):
        shifts[i].wait_recv()
        return work[upper_slot, rows, :], work[lower_slot, rows, :]

    statistics(1, fetch_shifted)
    copy = remote(
        gram_out.at[1, 1 - core], gram_in.at[2], gram_send.at[2], gram_recv.at[2], partner, col
    )
    copy.start()
    pending.append(copy)
    copy.wait_recv()
    total, copies = reduce_line(1, gram_out[1, core] + gram_in[2])
    pending += copies
    p, copy = coupling(1, total)
    pending.append(copy)
    out_p[...] = p
    for copy in pending:
        copy.wait_send()


def finish(work, p_ref, out_upper, out_lower, stage, sems):
    depth, width = out_upper.shape
    chunk = depth // CHUNKS
    odd = lax.rem(lax.axis_index("col"), 2)
    upper_slot, lower_slot = 2 - 2 * odd, 1 + odd
    parts = split(rotation(p_ref[...]))
    copies = []
    for i in range(CHUNKS):
        rows = pl.ds(i * chunk, chunk)
        y = turn(work[upper_slot, rows, :], work[lower_slot, rows, :], parts)
        for which, out in enumerate((out_upper, out_lower)):
            stage[which, rows, :] = y[:, which * width : (which + 1) * width]
            copies.append(pltpu.make_async_copy(stage.at[which, rows], out.at[rows], sems.at[which, i]))
            copies[-1].start()
    for copy in copies:
        copy.wait()


def shards(n_row, n_col, upper_blocks, lower_blocks):
    depth, width = upper_blocks.shape
    half = width // 2
    n_line = n_row // 2
    out = jax.ShapeDtypeStruct((depth, width), F32)
    dma = pltpu.SemaphoreType.DMA
    work, p = pl.pallas_call(
        functools.partial(kernel, n_row, n_col),
        out_shape=(pltpu.VMEM((3, depth, width), F32), pltpu.VMEM((width, width), F32)),
        in_specs=[pl.BlockSpec(memory_space=pl.ANY)] * 2,
        out_specs=(pl.BlockSpec(memory_space=pltpu.VMEM),) * 2,
        scratch_shapes=[
            pltpu.VMEM((2, depth, width), F32),
            pltpu.VMEM((2, depth, width), F32),
            pltpu.VMEM((ROUNDS, 2, half + 8, width), F32),
            pltpu.VMEM((3, half + 8, width), F32),
            pltpu.VMEM((ROUNDS, half + 8, width), F32),
            pltpu.VMEM((ROUNDS, n_line - 1, half + 8, width), F32),
            pltpu.VMEM((ROUNDS, 2, half, width), F32),
            dma((2, CHUNKS)),
            dma((2, CHUNKS)),
            dma((3,)),
            dma((3,)),
            dma((ROUNDS, n_line - 1)),
            dma((ROUNDS, n_line - 1)),
            dma((ROUNDS,)),
            dma((ROUNDS,)),
            dma((CHUNKS,)),
            dma((CHUNKS,)),
            dma((2, CHUNKS)),
        ],
        compiler_params=pltpu.CompilerParams(collective_id=0, has_side_effects=True),
    )(upper_blocks, lower_blocks)
    return pl.pallas_call(
        finish,
        out_shape=(out, out),
        in_specs=[pl.BlockSpec(memory_space=pltpu.VMEM)] * 2,
        out_specs=(pl.BlockSpec(memory_space=pl.ANY),) * 2,
        scratch_shapes=[pltpu.VMEM((2, depth, width), F32), dma((2, CHUNKS))],
    )(*(pltpu.with_memory_space_constraint(x, pltpu.VMEM) for x in (work, p)))


def solution(mesh):
    placed = (P("row", "col"), P("row", "col"))
    return jax.shard_map(
        functools.partial(shards, mesh.shape["row"], mesh.shape["col"]),
        mesh=mesh,
        in_specs=placed,
        out_specs=(P("row", "col"), P("row", "col")),
        check_vma=False,
    )
```

```python
import functools

import jax
import jax.numpy as jnp
from jax import lax
from jax.experimental import pallas as pl
from jax.experimental.pallas import tpu as pltpu
from jax.sharding import PartitionSpec as P

ROUNDS = 2
LOADS = 2
SWAPS = 2
SHIFTS = 4
STORES = 4
MESH = pl.DeviceIdType.MESH
F32 = jnp.float32
BF16 = jnp.bfloat16


def split(x):
    high = x.astype(BF16)
    low = (x - high.astype(F32)).astype(BF16)
    return high, low


def split_three(x):
    high = x.astype(BF16)
    rest = x - high.astype(F32)
    middle = rest.astype(BF16)
    return high, middle, (rest - middle.astype(F32)).astype(BF16)


def fast_dot(a, b):
    return jnp.dot(a, b, preferred_element_type=F32)


def exact_dot(a, b):
    width = b.shape[1]
    (a0, a1, a2), (b0, b1, b2) = split_three(a), split_three(b)
    upper = jnp.concatenate([b0, b1], axis=1)
    lower = jnp.concatenate([b1, b0], axis=1)
    large = fast_dot(jnp.concatenate([a0, a1], axis=1), jnp.concatenate([upper, lower], axis=0))
    small = fast_dot(jnp.concatenate([a0, a2], axis=1), jnp.concatenate([b2, b0], axis=0))
    return large[:, :width] + (large[:, width:] + small)


def gram(upper, lower):
    width = upper.shape[1]
    left = jnp.concatenate(split(upper), axis=1)
    right = jnp.concatenate(split(lower), axis=1)
    q = lax.dot_general(
        left, right, (((0,), (0,)), ((), ())), preferred_element_type=F32
    )
    return q[:width, :width] + (q[:width, width:] + q[width:, :width])


def step_count(width):
    square = (width / 4.0) ** 2
    spread = 0.5 * square / (1.0 + 0.5 * square)
    steps = 0
    while spread > 1e-3:
        spread = spread * spread / (2.0 - spread * spread)
        steps += 1
    return steps


def rotation(p):
    width = p.shape[0]
    rows = lax.broadcasted_iota(jnp.int32, (width, width), 0)
    lanes = lax.broadcasted_iota(jnp.int32, (width, width), 1)
    eye = (rows == lanes).astype(F32)
    s = exact_dot(p, p.T)
    total = jnp.sum(jnp.sum(p * p, axis=0, keepdims=True), axis=1, keepdims=True)
    total = jnp.broadcast_to(total, (1, width))
    scale = 1.0 / (1.0 + 0.5 * total)
    spread = 0.5 * total * scale
    e = spread * eye - scale * s
    x = None
    steps = step_count(width)
    for step in range(steps):
        square = spread * spread
        gain = 2.0 / (2.0 - square)
        spread = 0.5 * square * gain
        if step == 0:
            x = (gain * scale) * (eye + e)
            squared = exact_dot(e, e)
        elif step < steps - 1:
            squared = exact_dot(e, e)
            x = gain * (x + exact_dot(x, e))
        else:
            x = gain * (x + exact_dot(x, e))
        if step < steps - 1:
            e = gain * squared - spread * eye
    e = (eye - x) - exact_dot(s, x)
    x = x + exact_dot(x, e)
    ap = exact_dot(x, p)
    cross = 2.0 * ap
    keep_upper = 2.0 * x - eye
    keep_lower = eye - exact_dot(p.T, cross)
    top = jnp.concatenate([keep_upper, cross], axis=1)
    bottom = jnp.concatenate([-cross.T, keep_lower], axis=1)
    return jnp.concatenate([top, bottom], axis=0)


def turn(upper, lower, parts):
    high, low = split(jnp.concatenate([upper, lower], axis=1))
    w_high, w_low = parts
    return fast_dot(high, w_high) + (fast_dot(low, w_high) + fast_dot(high, w_low))


def kernel(
    n_row, n_col, upper_hbm, lower_hbm, work, out_p,
    loaded, swapped, gram_out, gram_in, line_out, line_in, pair,
    swap_send, swap_recv, gram_send, gram_recv, line_send, line_recv,
    pair_send, pair_recv, shift_send, shift_recv, load_sem,
):
    depth, width = upper_hbm.shape
    upper_ref, lower_ref = loaded.at[0], loaded.at[1]
    half = width // 2
    n_line = n_row // 2
    row_total = float(depth * n_row)
    row, col = lax.axis_index("row"), lax.axis_index("col")
    core = lax.rem(row, 2)
    chip_row = row - core
    partner = chip_row + 1 - core
    odd = lax.rem(col, 2)
    beside = col + 1 - 2 * odd
    ahead = lax.rem(col + 2, n_col)
    behind = lax.rem(col + n_col - 2, n_col)
    shift_to = ahead + odd * (behind - ahead)

    def line_row(k):
        return lax.rem(row + 2 * k, n_row)

    def piece(i, count):
        return pl.ds(i * (depth // count), depth // count)

    loads = []
    for i in range(LOADS):
        rows = piece(i, LOADS)
        for which, ref in enumerate((upper_hbm, lower_hbm)):
            loads.append(pltpu.make_async_copy(ref.at[rows], loaded.at[which, rows], load_sem.at[which, i]))
            loads[-1].start()
    barrier = pltpu.get_barrier_semaphore()
    greeted = [(chip_row, beside), (chip_row + 1, beside), (partner, col)]
    greeted += [(line_row(k), col) for k in range(1, n_line)]
    greeted += [(row, ahead)] + ([] if n_col == 4 else [(row, behind)])
    for r, c in greeted:
        pl.semaphore_signal(barrier, inc=1, device_id={"row": r, "col": c}, device_id_type=MESH)

    def remote(src, dst, send, recv, r, c):
        return pltpu.make_async_remote_copy(
            src_ref=src, dst_ref=dst, send_sem=send, recv_sem=recv,
            device_id={"row": r, "col": c}, device_id_type=MESH,
        )

    def put_statistics(index, g, upper_sums, lower_sums):
        which = lax.broadcasted_iota(jnp.int32, (8, width), 0)
        norms = jnp.where(which == 0, upper_sums, jnp.where(which == 1, lower_sums, 0.0))
        for k in range(2):
            gram_out[index, k, :half, :] = g[k * half : (k + 1) * half]
            gram_out[index, k, half:, :] = norms

    def reduce_line(index, own):
        line_out[index] = own
        copies = []
        for k in range(1, n_line):
            copies.append(
                remote(
                    line_out.at[index], line_in.at[index, k - 1],
                    line_send.at[index, k - 1], line_recv.at[index, k - 1], line_row(k), col,
                )
            )
            copies[-1].start()
        total = own
        for k in range(1, n_line):
            copies[k - 1].wait_recv()
            total = total + line_in[index, k - 1]
        return total, copies

    def coupling(index, total):
        total = total / row_total
        a_row, b = total[half : half + 1], total[half + 1 : half + 2]
        i = lax.broadcasted_iota(jnp.int32, (half, width), 0) + core * half
        j = lax.broadcasted_iota(jnp.int32, (half, width), 1)
        a = jnp.sum(jnp.where(i == j, a_row, 0.0), axis=1, keepdims=True)
        gap, both = a - b, a + b
        share = -total[:half] * gap / (2.0 * gap * gap + 0.5 * both * both + 1e-05)
        pair[index, core] = share
        copy = remote(
            pair.at[index, core], pair.at[index, core],
            pair_send.at[index], pair_recv.at[index], partner, col,
        )
        copy.start()
        copy.wait_recv()
        return pair[index].reshape(width, width), copy

    pending = []

    def statistics(index, count, fetch):
        g, upper_sums, lower_sums = 0.0, 0.0, 0.0
        for i in range(count):
            upper, lower = fetch(i, piece(i, count))
            g = g + gram(upper, lower)
            upper_sums = upper_sums + jnp.sum(upper * upper, axis=0, keepdims=True)
            lower_sums = lower_sums + jnp.sum(lower * lower, axis=0, keepdims=True)
        put_statistics(index, g, upper_sums, lower_sums)

    def fetch_loaded(i, rows):
        loads[2 * i].wait()
        loads[2 * i + 1].wait()
        return loaded[0, rows, :], loaded[1, rows, :]

    statistics(0, LOADS, fetch_loaded)
    pl.semaphore_wait(barrier, len(greeted))

    copies = []
    for k in range(2):
        copies.append(
            remote(
                gram_out.at[0, k], gram_in.at[core], gram_send.at[k], gram_recv.at[core],
                chip_row + k, beside,
            )
        )
        copies[-1].start()
    pending += copies
    swaps = []
    for i in range(SWAPS):
        rows = piece(i, SWAPS)
        for which, ref in enumerate((upper_ref, lower_ref)):
            swaps.append(
                remote(
                    ref.at[rows], swapped.at[which, rows],
                    swap_send.at[which, i], swap_recv.at[which, i], row, beside,
                )
            )
            swaps[-1].start()
    pending += swaps
    for k in range(2):
        pltpu.make_async_remote_copy(
            src_ref=gram_out.at[0, k], dst_ref=gram_in.at[k], send_sem=gram_send.at[k],
            recv_sem=gram_recv.at[k], device_id={"row": row, "col": beside}, device_id_type=MESH,
        ).wait_recv()
    total, copies = reduce_line(0, gram_in[0] + gram_in[1])
    pending += copies
    p, copy = coupling(0, total)
    pending.append(copy)
    parts = split(rotation(p))

    shifts = []
    for i in range(SHIFTS):
        rows = piece(i, SHIFTS)
        if i % (SHIFTS // SWAPS) == 0:
            swaps[2 * (i * SWAPS // SHIFTS)].wait_recv()
            swaps[2 * (i * SWAPS // SHIFTS) + 1].wait_recv()
        y = turn(swapped[0, rows, :], swapped[1, rows, :], parts)
        work[0, rows, :] = y[:, :width]
        work[1, rows, :] = y[:, width:]
        shifts.append(
            remote(
                work.at[odd, rows], work.at[2, rows], shift_send.at[i], shift_recv.at[i],
                row, shift_to,
            )
        )
        shifts[-1].start()
    pending += shifts

    upper_slot, lower_slot = 2 - 2 * odd, 1 + odd

    def fetch_shifted(i, rows):
        shifts[i].wait_recv()
        return work[upper_slot, rows, :], work[lower_slot, rows, :]

    statistics(1, SHIFTS, fetch_shifted)
    copy = remote(
        gram_out.at[1, 1 - core], gram_in.at[2], gram_send.at[2], gram_recv.at[2], partner, col
    )
    copy.start()
    pending.append(copy)
    copy.wait_recv()
    total, copies = reduce_line(1, gram_out[1, core] + gram_in[2])
    pending += copies
    p, copy = coupling(1, total)
    pending.append(copy)
    out_p[...] = p
    for copy in pending:
        copy.wait_send()


def finish(work, p_ref, out_upper, out_lower, stage, sems):
    depth, width = out_upper.shape
    chunk = depth // STORES
    odd = lax.rem(lax.axis_index("col"), 2)
    upper_slot, lower_slot = 2 - 2 * odd, 1 + odd
    parts = split(rotation(p_ref[...]))
    copies = []
    for i in range(STORES):
        rows = pl.ds(i * chunk, chunk)
        y = turn(work[upper_slot, rows, :], work[lower_slot, rows, :], parts)
        for which, out in enumerate((out_upper, out_lower)):
            stage[which, rows, :] = y[:, which * width : (which + 1) * width]
            copies.append(pltpu.make_async_copy(stage.at[which, rows], out.at[rows], sems.at[which, i]))
            copies[-1].start()
    for copy in copies:
        copy.wait()


def shards(n_row, n_col, upper_blocks, lower_blocks):
    depth, width = upper_blocks.shape
    half = width // 2
    n_line = n_row // 2
    out = jax.ShapeDtypeStruct((depth, width), F32)
    dma = pltpu.SemaphoreType.DMA
    work, p = pl.pallas_call(
        functools.partial(kernel, n_row, n_col),
        out_shape=(pltpu.VMEM((3, depth, width), F32), pltpu.VMEM((width, width), F32)),
        in_specs=[pl.BlockSpec(memory_space=pl.ANY)] * 2,
        out_specs=(pl.BlockSpec(memory_space=pltpu.VMEM),) * 2,
        scratch_shapes=[
            pltpu.VMEM((2, depth, width), F32),
            pltpu.VMEM((2, depth, width), F32),
            pltpu.VMEM((ROUNDS, 2, half + 8, width), F32),
            pltpu.VMEM((3, half + 8, width), F32),
            pltpu.VMEM((ROUNDS, half + 8, width), F32),
            pltpu.VMEM((ROUNDS, n_line - 1, half + 8, width), F32),
            pltpu.VMEM((ROUNDS, 2, half, width), F32),
            dma((2, SWAPS)),
            dma((2, SWAPS)),
            dma((3,)),
            dma((3,)),
            dma((ROUNDS, n_line - 1)),
            dma((ROUNDS, n_line - 1)),
            dma((ROUNDS,)),
            dma((ROUNDS,)),
            dma((SHIFTS,)),
            dma((SHIFTS,)),
            dma((2, LOADS)),
        ],
        compiler_params=pltpu.CompilerParams(collective_id=0, has_side_effects=True),
    )(upper_blocks, lower_blocks)
    return pl.pallas_call(
        finish,
        out_shape=(out, out),
        in_specs=[pl.BlockSpec(memory_space=pltpu.VMEM)] * 2,
        out_specs=(pl.BlockSpec(memory_space=pl.ANY),) * 2,
        scratch_shapes=[pltpu.VMEM((2, depth, width), F32), dma((2, STORES))],
    )(*(pltpu.with_memory_space_constraint(x, pltpu.VMEM) for x in (work, p)))


def solution(mesh):
    placed = (P("row", "col"), P("row", "col"))
    return jax.shard_map(
        functools.partial(shards, mesh.shape["row"], mesh.shape["col"]),
        mesh=mesh,
        in_specs=placed,
        out_specs=(P("row", "col"), P("row", "col")),
        check_vma=False,
    )
```

```python
import functools

import jax
import jax.numpy as jnp
from jax import lax
from jax.experimental import pallas as pl
from jax.experimental.pallas import tpu as pltpu
from jax.sharding import PartitionSpec as P

ROUNDS = 2
LOADS = 2
SWAPS = 2
SHIFTS = 4
STORES = 4
MESH = pl.DeviceIdType.MESH
F32 = jnp.float32
BF16 = jnp.bfloat16


def split(x):
    high = x.astype(BF16)
    low = (x - high.astype(F32)).astype(BF16)
    return high, low


def split_three(x):
    high = x.astype(BF16)
    rest = x - high.astype(F32)
    middle = rest.astype(BF16)
    return high, middle, (rest - middle.astype(F32)).astype(BF16)


def fast_dot(a, b):
    return jnp.dot(a, b, preferred_element_type=F32)


def exact_dot(a, b):
    width = b.shape[1]
    (a0, a1, a2), (b0, b1, b2) = split_three(a), split_three(b)
    upper = jnp.concatenate([b0, b1], axis=1)
    lower = jnp.concatenate([b1, b0], axis=1)
    large = fast_dot(jnp.concatenate([a0, a1], axis=1), jnp.concatenate([upper, lower], axis=0))
    small = fast_dot(jnp.concatenate([a0, a2], axis=1), jnp.concatenate([b2, b0], axis=0))
    return large[:, :width] + (large[:, width:] + small)


def gram(upper, lower):
    width = upper.shape[1]
    left = jnp.concatenate(split(upper), axis=1)
    right = jnp.concatenate(split(lower), axis=1)
    q = lax.dot_general(
        left, right, (((0,), (0,)), ((), ())), preferred_element_type=F32
    )
    return q[:width, :width] + (q[:width, width:] + q[width:, :width])


def step_count(width):
    square = (width / 4.0) ** 2
    spread = 0.5 * square / (1.0 + 0.5 * square)
    steps = 0
    while spread > 1e-3:
        spread = spread * spread / (2.0 - spread * spread)
        steps += 1
    return steps


def rotation(p):
    width = p.shape[0]
    rows = lax.broadcasted_iota(jnp.int32, (width, width), 0)
    lanes = lax.broadcasted_iota(jnp.int32, (width, width), 1)
    eye = (rows == lanes).astype(F32)
    s = exact_dot(p, p.T)
    total = jnp.sum(jnp.sum(p * p, axis=0, keepdims=True), axis=1, keepdims=True)
    total = jnp.broadcast_to(total, (1, width))
    scale = 1.0 / (1.0 + 0.5 * total)
    spread = 0.5 * total * scale
    e = spread * eye - scale * s
    x = None
    steps = step_count(width)
    for step in range(steps):
        square = spread * spread
        gain = 2.0 / (2.0 - square)
        spread = 0.5 * square * gain
        if step == 0:
            x = (gain * scale) * (eye + e)
            squared = exact_dot(e, e)
        elif step < steps - 1:
            squared = exact_dot(e, e)
            x = gain * (x + exact_dot(x, e))
        else:
            x = gain * (x + exact_dot(x, e))
        if step < steps - 1:
            e = gain * squared - spread * eye
    e = (eye - x) - exact_dot(s, x)
    x = x + exact_dot(x, e)
    ap = exact_dot(x, p)
    cross = 2.0 * ap
    keep_upper = 2.0 * x - eye
    keep_lower = eye - exact_dot(p.T, cross)
    top = jnp.concatenate([keep_upper, cross], axis=1)
    bottom = jnp.concatenate([-cross.T, keep_lower], axis=1)
    return jnp.concatenate([top, bottom], axis=0)


def turn(upper, lower, parts):
    high, low = split(jnp.concatenate([upper, lower], axis=1))
    w_high, w_low = parts
    return fast_dot(high, w_high) + (fast_dot(low, w_high) + fast_dot(high, w_low))


def kernel(
    n_row, n_col, upper_hbm, lower_hbm, work, out_p,
    loaded, swapped, gram_out, gram_in, line_out, line_in, pair,
    swap_send, swap_recv, gram_send, gram_recv, line_send, line_recv,
    pair_send, pair_recv, shift_send, shift_recv, load_sem,
):
    depth, width = upper_hbm.shape
    upper_ref, lower_ref = loaded.at[0], loaded.at[1]
    half = width // 2
    n_line = n_row // 2
    row_total = float(depth * n_row)
    row, col = lax.axis_index("row"), lax.axis_index("col")
    core = lax.rem(row, 2)
    chip_row = row - core
    partner = chip_row + 1 - core
    odd = lax.rem(col, 2)
    beside = col + 1 - 2 * odd
    ahead = lax.rem(col + 2, n_col)
    behind = lax.rem(col + n_col - 2, n_col)
    shift_to = ahead + odd * (behind - ahead)

    def line_row(k):
        return lax.rem(row + 2 * k, n_row)

    def piece(i, count):
        return pl.ds(i * (depth // count), depth // count)

    loads = []
    for i in range(LOADS):
        rows = piece(i, LOADS)
        for which, ref in enumerate((upper_hbm, lower_hbm)):
            loads.append(pltpu.make_async_copy(ref.at[rows], loaded.at[which, rows], load_sem.at[which, i]))
            loads[-1].start()
    barrier = pltpu.get_barrier_semaphore()
    greeted = [(chip_row, beside), (chip_row + 1, beside), (partner, col)]
    greeted += [(line_row(k), col) for k in range(1, n_line)]
    greeted += [(row, ahead)] + ([] if n_col == 4 else [(row, behind)])
    for r, c in greeted:
        pl.semaphore_signal(barrier, inc=1, device_id={"row": r, "col": c}, device_id_type=MESH)

    def remote(src, dst, send, recv, r, c):
        return pltpu.make_async_remote_copy(
            src_ref=src, dst_ref=dst, send_sem=send, recv_sem=recv,
            device_id={"row": r, "col": c}, device_id_type=MESH,
        )

    def put_statistics(index, g, upper_sums, lower_sums):
        which = lax.broadcasted_iota(jnp.int32, (8, width), 0)
        norms = jnp.where(which == 0, upper_sums, jnp.where(which == 1, lower_sums, 0.0))
        for k in range(2):
            gram_out[index, k, :half, :] = g[k * half : (k + 1) * half]
            gram_out[index, k, half:, :] = norms

    def reduce_line(index, own):
        line_out[index] = own
        copies = []
        for k in range(1, n_line):
            copies.append(
                remote(
                    line_out.at[index], line_in.at[index, k - 1],
                    line_send.at[index, k - 1], line_recv.at[index, k - 1], line_row(k), col,
                )
            )
            copies[-1].start()
        total = own
        for k in range(1, n_line):
            copies[k - 1].wait_recv()
            total = total + line_in[index, k - 1]
        return total, copies

    def coupling(index, total):
        pair[index, core] = total[:half]
        copy = remote(
            pair.at[index, core], pair.at[index, core],
            pair_send.at[index], pair_recv.at[index], partner, col,
        )
        copy.start()
        norms = total[half:] / row_total
        a_row, b = norms[:1], norms[1:2]
        a = jnp.broadcast_to(a_row, (width, width)).T
        gap, both = a - b, a + b
        factor = -gap / (2.0 * gap * gap + 0.5 * both * both + 1e-05)
        copy.wait_recv()
        cross_gram = pair[index].reshape(width, width) / row_total
        return cross_gram * factor, copy

    pending = []

    def statistics(index, count, fetch):
        g, upper_sums, lower_sums = 0.0, 0.0, 0.0
        for i in range(count):
            upper, lower = fetch(i, piece(i, count))
            g = g + gram(upper, lower)
            upper_sums = upper_sums + jnp.sum(upper * upper, axis=0, keepdims=True)
            lower_sums = lower_sums + jnp.sum(lower * lower, axis=0, keepdims=True)
        put_statistics(index, g, upper_sums, lower_sums)

    def fetch_loaded(i, rows):
        loads[2 * i].wait()
        loads[2 * i + 1].wait()
        return loaded[0, rows, :], loaded[1, rows, :]

    statistics(0, LOADS, fetch_loaded)
    pl.semaphore_wait(barrier, len(greeted))

    copies = []
    for k in range(2):
        copies.append(
            remote(
                gram_out.at[0, k], gram_in.at[core], gram_send.at[k], gram_recv.at[core],
                chip_row + k, beside,
            )
        )
        copies[-1].start()
    pending += copies
    swaps = []
    for i in range(SWAPS):
        rows = piece(i, SWAPS)
        for which, ref in enumerate((upper_ref, lower_ref)):
            swaps.append(
                remote(
                    ref.at[rows], swapped.at[which, rows],
                    swap_send.at[which, i], swap_recv.at[which, i], row, beside,
                )
            )
            swaps[-1].start()
    pending += swaps
    for k in range(2):
        pltpu.make_async_remote_copy(
            src_ref=gram_out.at[0, k], dst_ref=gram_in.at[k], send_sem=gram_send.at[k],
            recv_sem=gram_recv.at[k], device_id={"row": row, "col": beside}, device_id_type=MESH,
        ).wait_recv()
    total, copies = reduce_line(0, gram_in[0] + gram_in[1])
    pending += copies
    p, copy = coupling(0, total)
    pending.append(copy)
    parts = split(rotation(p))

    shifts = []
    for i in range(SHIFTS):
        rows = piece(i, SHIFTS)
        if i % (SHIFTS // SWAPS) == 0:
            swaps[2 * (i * SWAPS // SHIFTS)].wait_recv()
            swaps[2 * (i * SWAPS // SHIFTS) + 1].wait_recv()
        y = turn(swapped[0, rows, :], swapped[1, rows, :], parts)
        work[0, rows, :] = y[:, :width]
        work[1, rows, :] = y[:, width:]
        shifts.append(
            remote(
                work.at[odd, rows], work.at[2, rows], shift_send.at[i], shift_recv.at[i],
                row, shift_to,
            )
        )
        shifts[-1].start()
    pending += shifts

    upper_slot, lower_slot = 2 - 2 * odd, 1 + odd

    def fetch_shifted(i, rows):
        shifts[i].wait_recv()
        return work[upper_slot, rows, :], work[lower_slot, rows, :]

    statistics(1, SHIFTS, fetch_shifted)
    copy = remote(
        gram_out.at[1, 1 - core], gram_in.at[2], gram_send.at[2], gram_recv.at[2], partner, col
    )
    copy.start()
    pending.append(copy)
    copy.wait_recv()
    total, copies = reduce_line(1, gram_out[1, core] + gram_in[2])
    pending += copies
    p, copy = coupling(1, total)
    pending.append(copy)
    out_p[...] = p
    for copy in pending:
        copy.wait_send()


def finish(work, p_ref, out_upper, out_lower, stage, sems):
    depth, width = out_upper.shape
    chunk = depth // STORES
    odd = lax.rem(lax.axis_index("col"), 2)
    upper_slot, lower_slot = 2 - 2 * odd, 1 + odd
    parts = split(rotation(p_ref[...]))
    copies = []
    for i in range(STORES):
        rows = pl.ds(i * chunk, chunk)
        y = turn(work[upper_slot, rows, :], work[lower_slot, rows, :], parts)
        for which, out in enumerate((out_upper, out_lower)):
            stage[which, rows, :] = y[:, which * width : (which + 1) * width]
            copies.append(pltpu.make_async_copy(stage.at[which, rows], out.at[rows], sems.at[which, i]))
            copies[-1].start()
    for copy in copies:
        copy.wait()


def shards(n_row, n_col, upper_blocks, lower_blocks):
    depth, width = upper_blocks.shape
    half = width // 2
    n_line = n_row // 2
    out = jax.ShapeDtypeStruct((depth, width), F32)
    dma = pltpu.SemaphoreType.DMA
    work, p = pl.pallas_call(
        functools.partial(kernel, n_row, n_col),
        out_shape=(pltpu.VMEM((3, depth, width), F32), pltpu.VMEM((width, width), F32)),
        in_specs=[pl.BlockSpec(memory_space=pl.ANY)] * 2,
        out_specs=(pl.BlockSpec(memory_space=pltpu.VMEM),) * 2,
        scratch_shapes=[
            pltpu.VMEM((2, depth, width), F32),
            pltpu.VMEM((2, depth, width), F32),
            pltpu.VMEM((ROUNDS, 2, half + 8, width), F32),
            pltpu.VMEM((3, half + 8, width), F32),
            pltpu.VMEM((ROUNDS, half + 8, width), F32),
            pltpu.VMEM((ROUNDS, n_line - 1, half + 8, width), F32),
            pltpu.VMEM((ROUNDS, 2, half, width), F32),
            dma((2, SWAPS)),
            dma((2, SWAPS)),
            dma((3,)),
            dma((3,)),
            dma((ROUNDS, n_line - 1)),
            dma((ROUNDS, n_line - 1)),
            dma((ROUNDS,)),
            dma((ROUNDS,)),
            dma((SHIFTS,)),
            dma((SHIFTS,)),
            dma((2, LOADS)),
        ],
        compiler_params=pltpu.CompilerParams(collective_id=0, has_side_effects=True),
    )(upper_blocks, lower_blocks)
    return pl.pallas_call(
        finish,
        out_shape=(out, out),
        in_specs=[pl.BlockSpec(memory_space=pltpu.VMEM)] * 2,
        out_specs=(pl.BlockSpec(memory_space=pl.ANY),) * 2,
        scratch_shapes=[pltpu.VMEM((2, depth, width), F32), dma((2, STORES))],
    )(*(pltpu.with_memory_space_constraint(x, pltpu.VMEM) for x in (work, p)))


def solution(mesh):
    placed = (P("row", "col"), P("row", "col"))
    return jax.shard_map(
        functools.partial(shards, mesh.shape["row"], mesh.shape["col"]),
        mesh=mesh,
        in_specs=placed,
        out_specs=(P("row", "col"), P("row", "col")),
        check_vma=False,
    )
```
